32 devices in a mesh: clip: 2 (over y), tm: 4 (over z), band: 2 (over x), head: 2 (over core).
Axes of the slice: x: 2, y: 2, z: 4, core: 2. Of those that a mesh axis runs over, the one named last changes fastest.
Arguments:
- queries: bfloat16 [8, 2, 256, 1536], P(('clip', 'tm'), 'band', None, 'head'), parts along dimension 0, may hold values from -6 to 6
- keys: bfloat16 [8, 2, 256, 1536], P(('clip', 'tm'), 'band', None, 'head'), parts along dimension 0, may hold values from -6 to 6
- values: bfloat16 [8, 2, 256, 1536], P(('clip', 'tm'), 'band', None, 'head'), parts along dimension 0, may hold values from -6 to 6
- adj_mask: int32 [8, 2, 2, 2], P(('clip', 'tm'), 'band'), parts along dimension 0, may hold values from 0 to 1, as said below
- border_blocks: int32 [8, 2, 2, 1], P(('clip', 'tm'), 'band'), parts along dimension 0, may hold values from 0 to 1
Outputs:
- attended: bfloat16 [8, 2, 256, 1536], P(('clip', 'tm'), 'band', None, 'head'), parts along dimension 0
The draws below stay inside these ranges and needn't reach their ends.
There are 2 independent parts, one for each index of `clip`. The reference program is written for one: setup_inputs(seed, part) draws one part's arguments, and reference() takes and returns one part's arrays. A program takes and returns all parts, laid end to end along the dimension named above; each array names one. Nothing has to cross between parts.
Inputs may be any that keep to these rules, and one draw needn't show every extreme that they name: `adj_mask`: for each slab, band and direction exactly 1 of the 2 entries are 1.
All inputs are finite; a program needn't handle non-finite values.
Results may differ from the reference program's by a relative error of at most 0.0043.
Values may be sent and summed in bfloat16 or wider, within the bound.
A program may use at most 64 MiB of HBM per device.

```python
import math
import jax
import jax.numpy as jnp
from jax import lax

SLABS = 4
BANDS = 2
ROWS = 256
BLK = 128
KB = 2
BSEL = 1
HEADS = 12
HD = 128


def draw_pair(key):
    array_shape = (SLABS, BANDS, ROWS, HEADS * HD)
    first_key, second_key = jax.random.split(key, 2)
    query_field = jnp.clip(jax.random.normal(first_key, array_shape, jnp.float32), -6.0, 6.0)
    key_field = jnp.clip(jax.random.normal(second_key, array_shape, jnp.float32), -6.0, 6.0)
    return (query_field, key_field)


def draw_queries(key, part):
    return draw_pair(jax.random.fold_in(key, 11))[0].astype(jnp.bfloat16)


def draw_keys(key, part):
    return draw_pair(jax.random.fold_in(key, 11))[1].astype(jnp.bfloat16)


def block_orders(key):
    streams = jax.random.split(key, SLABS * BANDS * 2)
    return jax.vmap(lambda stream: jax.random.permutation(stream, KB))(streams)


def draw_adj_mask(key, part):
    orders = block_orders(jax.random.fold_in(key, 23))
    return (orders < KB // 2).astype(jnp.int32).reshape(SLABS, BANDS, 2, KB)


def draw_border_blocks(key, part):
    orders = block_orders(jax.random.fold_in(key, 37))
    return orders[:, :BSEL].astype(jnp.int32).reshape(SLABS, BANDS, 2, BSEL)


def levels(key, extent, cuts, low, high):
    level, own = 1.0, jax.random.fold_in(key, 6)
    for dim, shards_of in cuts:
        heights = jnp.exp(jax.random.uniform(jax.random.fold_in(own, dim), (shards_of,), jnp.float32, low / len(cuts), high / len(cuts)))
        level = level * jnp.repeat(heights, extent[dim] // shards_of).reshape([-1 if axis == dim else 1 for axis in range(len(extent))])
    return level


def normal_values(rng, dims, deviation, most, cuts=(), kind=jnp.bfloat16):
    values = deviation * jax.random.normal(rng, dims, jnp.float32)
    if cuts:
        values = values * levels(rng, dims, cuts, -0.22, 0.18)
    return jnp.clip(values, -most, most).astype(kind)


def setup_inputs(seed: int = 0, part: int = 0) -> dict:
    seeds = jax.random.split(jax.random.key(seed), 6)
    part_keys = jax.random.split(jax.random.fold_in(seeds[5], part), 6)
    queries = draw_queries(jax.random.fold_in(jax.random.fold_in(seeds[5], part), 71), part)
    keys = draw_keys(jax.random.fold_in(jax.random.fold_in(seeds[5], part), 71), part)
    values = normal_values(part_keys[2], (SLABS, BANDS, ROWS, HEADS * HD), 1.0, 6.0, ((0, 4), (1, 2), (3, 2)))
    adj_mask = draw_adj_mask(jax.random.fold_in(jax.random.fold_in(seeds[5], part), 71), part)
    border_blocks = draw_border_blocks(jax.random.fold_in(jax.random.fold_in(seeds[5], part), 71), part)
    return dict(queries=queries, keys=keys, values=values, adj_mask=adj_mask, border_blocks=border_blocks)


masked_score = -1e+30

def attend(query_rows, key_rows, value_rows, bias):
    query_heads = query_rows.reshape(query_rows.shape[0], HEADS, HD).astype(jnp.float32)
    key_heads = key_rows.reshape(key_rows.shape[0], HEADS, HD).astype(jnp.float32)
    value_heads = value_rows.reshape(value_rows.shape[0], HEADS, HD).astype(jnp.float32)
    scores = jnp.einsum('qhd,khd->hqk', query_heads, key_heads) * (1.0 / math.sqrt(HD)) + bias
    maxima = lax.optimization_barrier(jnp.max(scores, axis=2))
    weights = jnp.exp(scores - maxima[:, :, None])
    totals = lax.optimization_barrier(jnp.sum(weights, axis=2))
    rounded = lax.optimization_barrier(weights.astype(jnp.bfloat16)).astype(jnp.float32)
    output = jnp.einsum('hqk,khd->qhd', rounded, value_heads)
    return (maxima, totals, output)

def combine_sources(pieces):
    maxima = jnp.stack([piece[0] for piece in pieces])
    largest = lax.optimization_barrier(jnp.max(maxima, axis=0))
    factors = jnp.exp(maxima - largest)
    numerator = factors[0].T[:, :, None] * pieces[0][2]
    for number in range(1, len(pieces)):
        numerator = numerator + factors[number].T[:, :, None] * pieces[number][2]
    denominator = lax.optimization_barrier(jnp.sum(factors * jnp.stack([piece[1] for piece in pieces]), axis=0))
    return numerator / denominator.T[:, :, None]

def reference(queries, keys, values, adj_mask, border_blocks):

    def one_device(device_index):
        slab_index = device_index // BANDS
        band_index = device_index % BANDS
        prev_slab = jnp.maximum(slab_index - 1, 0)
        next_slab = jnp.minimum(slab_index + 1, SLABS - 1)
        lower_band = jnp.maximum(band_index - 1, 0)
        upper_band = jnp.minimum(band_index + 1, BANDS - 1)
        query_rows = queries[slab_index, band_index]
        own_piece = attend(query_rows, keys[slab_index, band_index], values[slab_index, band_index], jnp.zeros((ROWS,), jnp.float32))
        prev_bias = jnp.where(jnp.repeat(adj_mask[prev_slab, band_index, 0] == 1, BLK) & (slab_index > 0), 0.0, masked_score).astype(jnp.float32)
        prev_piece = attend(query_rows, keys[prev_slab, band_index], values[prev_slab, band_index], prev_bias)
        next_bias = jnp.where(jnp.repeat(adj_mask[next_slab, band_index, 1] == 1, BLK) & (slab_index < SLABS - 1), 0.0, masked_score).astype(jnp.float32)
        next_piece = attend(query_rows, keys[next_slab, band_index], values[next_slab, band_index], next_bias)

        def picked_rows(source, band_from, direction):
            chosen = border_blocks[slab_index, band_from, direction]
            return source[slab_index, band_from].reshape(KB, BLK, HEADS * HD)[chosen].reshape(BSEL * BLK, HEADS * HD)
        rim_rows = BSEL * BLK
        lower_bias = jnp.where(band_index > 0, jnp.zeros((rim_rows,), jnp.float32), jnp.full((rim_rows,), masked_score, jnp.float32))
        upper_bias = jnp.where(band_index < BANDS - 1, jnp.zeros((rim_rows,), jnp.float32), jnp.full((rim_rows,), masked_score, jnp.float32))
        lower_piece = attend(query_rows, picked_rows(keys, lower_band, 1), picked_rows(values, lower_band, 1), lower_bias)
        upper_piece = attend(query_rows, picked_rows(keys, upper_band, 0), picked_rows(values, upper_band, 0), upper_bias)
        merged = combine_sources([own_piece, prev_piece, next_piece, lower_piece, upper_piece])
        return merged.reshape(ROWS, HEADS * HD).astype(jnp.bfloat16)
    results = lax.map(one_device, jnp.arange(SLABS * BANDS, dtype=jnp.int32))
    return results.reshape(SLABS, BANDS, ROWS, HEADS * HD)
```

```python
import functools
import math

import jax
import jax.numpy as jnp
from jax import lax
from jax.experimental import pallas as pl
from jax.experimental.pallas import tpu as pltpu
from jax.sharding import PartitionSpec as P

BLK = 128
HD = 128
GROUP = 2

masked_score = -1e30
SCALE2 = math.log2(math.e) / math.sqrt(HD)
MESH = pl.DeviceIdType.MESH


def routes(slab_count, band_count):
    slab, band = lax.axis_index("tm"), lax.axis_index("band")
    found = []
    if slab_count > 1:
        found.append(({"tm": slab + 1}, slab < slab_count - 1, slab > 0, ("adj", 0)))
        found.append(({"tm": slab - 1}, slab > 0, slab < slab_count - 1, ("adj", 1)))
    if band_count == 2:
        found.append(({"band": 1 - band}, None, None, ("border", 1 - band)))
    elif band_count > 2:
        found.append(({"band": band + 1}, band < band_count - 1, band > 0, ("border", 1)))
        found.append(({"band": band - 1}, band > 0, band < band_count - 1, ("border", 0)))
    return found


def when(condition):
    return (lambda body: body()) if condition is None else pl.when(condition)


def weigh(query, key):
    scores = lax.dot_general(
        query, key, (((1,), (1,)), ((), ())), preferred_element_type=jnp.float32
    )
    return scores * SCALE2


def kernel(
    slab_count, band_count, q_hbm, k_hbm, v_hbm, adj_hbm, border_hbm, out_hbm,
    q_ref, k_ref, v_ref, adj_ref, border_ref, send_ref, recv_ref, acc_ref, weights_ref,
    gain_ref, out_ref, load_sem, store_sem, send_sem, recv_sem,
):
    plan = routes(slab_count, band_count)
    rows, width = q_ref.shape
    heads = width // HD
    groups = heads // GROUP

    barrier = pltpu.get_barrier_semaphore()
    for target, sends, _, _ in plan:
        @when(sends)
        def _():
            pl.semaphore_signal(barrier, inc=1, device_id=target, device_id_type=MESH)

    loads = []
    for number, (source, target) in enumerate(
        ((adj_hbm, adj_ref), (border_hbm, border_ref), (k_hbm, k_ref), (v_hbm, v_ref), (q_hbm, q_ref))
    ):
        copy = pltpu.make_async_copy(source, target, load_sem.at[number])
        copy.start()
        loads.append(copy)

    for slot, (_, _, comes, _) in enumerate(plan):
        if comes is not None:
            @pl.when(jnp.logical_not(comes))
            def _():
                recv_ref[slot] = jnp.zeros(recv_ref.shape[1:], recv_ref.dtype)

    loads[0].wait()
    loads[1].wait()
    starts = []
    for _, _, _, (kind, row) in plan:
        starts.append(adj_ref[row, 1] if kind == "adj" else border_ref[0, row])
    for part, (load, whole) in enumerate(((loads[2], k_ref), (loads[3], v_ref))):
        load.wait()
        for slot in range(len(plan)):
            for head in range(heads):
                send_ref[slot, part, head] = whole[
                    starts[slot], :, head * HD : (head + 1) * HD
                ]

    arrivals = sum(1 if comes is None else comes.astype(jnp.int32) for _, _, comes, _ in plan)
    pl.semaphore_wait(barrier, arrivals)

    def transfer(slot, part, group):
        at = (slot, part, pl.ds(group * GROUP, GROUP))
        return pltpu.make_async_remote_copy(
            src_ref=send_ref.at[at],
            dst_ref=recv_ref.at[at],
            send_sem=send_sem.at[slot, part, group],
            recv_sem=recv_sem.at[slot, part, group],
            device_id=plan[slot][0],
            device_id_type=MESH,
        )

    for part in range(2):
        for group in range(groups):
            for slot, (_, sends, _, _) in enumerate(plan):
                @when(sends)
                def _():
                    transfer(slot, part, group).start()

    loads[4].wait()
    own = []
    for head in range(heads):
        columns = slice(head * HD, (head + 1) * HD)
        scores = weigh(q_ref[:, columns], k_ref[:, :, columns].reshape(rows, HD))
        most = jnp.max(scores, axis=1, keepdims=True)
        weights = jnp.exp2(scores - most)
        total = jnp.sum(weights, axis=1, keepdims=True)
        acc_ref[head] = jnp.dot(
            weights.astype(jnp.bfloat16), v_ref[:, :, columns].reshape(rows, HD), preferred_element_type=jnp.float32
        )
        own.append((most, total))

    for group in range(groups):
        for slot, (_, _, comes, _) in enumerate(plan):
            @when(comes)
            def _():
                transfer(slot, 0, group).wait_recv()
        for head in range(group * GROUP, (group + 1) * GROUP):
            columns = slice(head * HD, (head + 1) * HD)
            pieces = [own[head]]
            for slot, (_, _, comes, _) in enumerate(plan):
                scores = weigh(q_ref[:, columns], recv_ref[slot, 0, head])
                if comes is not None:
                    scores = scores + jnp.where(comes, 0.0, masked_score).astype(jnp.float32)
                most = jnp.max(scores, axis=1, keepdims=True)
                weights = jnp.exp2(scores - most)
                total = jnp.sum(weights, axis=1, keepdims=True)
                weights_ref[head, slot] = weights.astype(jnp.bfloat16)
                pieces.append((most, total))
            largest = functools.reduce(jnp.maximum, [most for most, _ in pieces])
            factors = [jnp.exp2(most - largest) for most, _ in pieces]
            denominator = sum(factor * total for factor, (_, total) in zip(factors, pieces))
            acc_ref[head] = acc_ref[head] * (factors[0] / denominator)
            for slot in range(len(plan)):
                gain_ref[head, slot] = jnp.broadcast_to(
                    factors[slot + 1] / denominator, (rows, HD)
                )

    stores = []
    for group in range(groups):
        for slot, (_, _, comes, _) in enumerate(plan):
            @when(comes)
            def _():
                transfer(slot, 1, group).wait_recv()
        for head in range(group * GROUP, (group + 1) * GROUP):
            result = acc_ref[head]
            for slot in range(len(plan)):
                result = result + gain_ref[head, slot] * jnp.dot(
                    weights_ref[head, slot], recv_ref[slot, 1, head], preferred_element_type=jnp.float32
                )
            out_ref[:, head * HD : (head + 1) * HD] = result.astype(out_ref.dtype)
        columns = pl.ds(group * GROUP * HD, GROUP * HD)
        store = pltpu.make_async_copy(
            out_ref.at[:, columns], out_hbm.at[:, columns], store_sem.at[group]
        )
        store.start()
        stores.append(store)

    for part in range(2):
        for group in range(groups):
            for slot, (_, sends, _, _) in enumerate(plan):
                @when(sends)
                def _():
                    transfer(slot, part, group).wait_send()
    for store in stores:
        store.wait()


def per_device(queries, keys, values, adj_mask, border_blocks):
    rows, width = queries.shape[2:]
    heads = width // HD
    slab_count, band_count = lax.axis_size("tm"), lax.axis_size("band")
    sources = (2 if slab_count > 1 else 0) + min(band_count - 1, 2)
    assert rows == 2 * BLK and adj_mask.shape[3] == 2 and border_blocks.shape[3] == 1
    block_sems = pltpu.SemaphoreType.DMA((sources, 2, heads // GROUP))
    attended = pl.pallas_call(
        functools.partial(kernel, slab_count, band_count),
        out_shape=jax.ShapeDtypeStruct((rows, width), jnp.bfloat16),
        in_specs=[pl.BlockSpec(memory_space=pl.ANY)] * 5,
        out_specs=pl.BlockSpec(memory_space=pl.ANY),
        scratch_shapes=[
            pltpu.VMEM((rows, width), jnp.bfloat16),
            pltpu.VMEM((rows // BLK, BLK, width), jnp.bfloat16),
            pltpu.VMEM((rows // BLK, BLK, width), jnp.bfloat16),
            pltpu.SMEM(adj_mask.shape[2:], jnp.int32),
            pltpu.SMEM(border_blocks.shape[:1:-1], jnp.int32),
            pltpu.VMEM((sources, 2, heads, BLK, HD), jnp.bfloat16),
            pltpu.VMEM((sources, 2, heads, BLK, HD), jnp.bfloat16),
            pltpu.VMEM((heads, rows, HD), jnp.float32),
            pltpu.VMEM((heads, sources, rows, BLK), jnp.bfloat16),
            pltpu.VMEM((heads, sources, rows, HD), jnp.float32),
            pltpu.VMEM((rows, width), jnp.bfloat16),
            pltpu.SemaphoreType.DMA((5,)),
            pltpu.SemaphoreType.DMA((heads // GROUP,)),
            block_sems,
            block_sems,
        ],
        compiler_params=pltpu.CompilerParams(collective_id=0, has_side_effects=True),
        name="radial_attention",
    )(
        queries[0, 0],
        keys.reshape(rows // BLK, BLK, width),
        values.reshape(rows // BLK, BLK, width),
        adj_mask[0, 0], border_blocks[0, 0].T,
    )
    return attended[None, None]


def solution(mesh):
    placed = (
        P(("clip", "tm"), "band", None, "head"),
        P(("clip", "tm"), "band", None, "head"),
        P(("clip", "tm"), "band", None, "head"),
        P(("clip", "tm"), "band", None, None),
        P(("clip", "tm"), "band", None, None),
    )
    return jax.shard_map(
        per_device,
        mesh=mesh,
        in_specs=placed,
        out_specs=P(("clip", "tm"), "band", None, "head"),
        check_vma=False,
    )
```

```python
import functools
import math

import jax
import jax.numpy as jnp
from jax import lax
from jax.experimental import pallas as pl
from jax.experimental.pallas import tpu as pltpu
from jax.sharding import PartitionSpec as P

BLK = 128
HD = 128
GROUP = 2

masked_score = -1e30
SCALE2 = math.log2(math.e) / math.sqrt(HD)
MESH = pl.DeviceIdType.MESH


def routes(slab_count, band_count):
    slab, band = lax.axis_index("tm"), lax.axis_index("band")
    found = []
    if slab_count > 1:
        found.append(({"tm": slab + 1}, slab < slab_count - 1, slab > 0, ("adj", 0)))
        found.append(({"tm": slab - 1}, slab > 0, slab < slab_count - 1, ("adj", 1)))
    if band_count == 2:
        found.append(({"band": 1 - band}, None, None, ("border", 1 - band)))
    elif band_count > 2:
        found.append(({"band": band + 1}, band < band_count - 1, band > 0, ("border", 1)))
        found.append(({"band": band - 1}, band > 0, band < band_count - 1, ("border", 0)))
    return found


def when(condition):
    return (lambda body: body()) if condition is None else pl.when(condition)


def weigh(query, key):
    scores = lax.dot_general(
        query, key, (((1,), (1,)), ((), ())), preferred_element_type=jnp.float32
    )
    return scores * SCALE2


def kernel(
    slab_count, band_count, q_hbm, k_hbm, v_hbm, adj_hbm, border_hbm, out_ref,
    q_ref, k_ref, v_ref, adj_ref, border_ref, send_ref, recv_ref, acc_ref, weights_ref,
    gain_ref, load_sem, send_sem, recv_sem,
):
    plan = routes(slab_count, band_count)
    rows, width = q_ref.shape
    heads = width // HD
    groups = heads // GROUP

    barrier = pltpu.get_barrier_semaphore()
    for target, sends, _, _ in plan:
        @when(sends)
        def _():
            pl.semaphore_signal(barrier, inc=1, device_id=target, device_id_type=MESH)

    loads = []
    for number, (source, target) in enumerate(
        ((adj_hbm, adj_ref), (border_hbm, border_ref), (k_hbm, k_ref), (v_hbm, v_ref), (q_hbm, q_ref))
    ):
        copy = pltpu.make_async_copy(source, target, load_sem.at[number])
        copy.start()
        loads.append(copy)

    for slot, (_, _, comes, _) in enumerate(plan):
        if comes is not None:
            @pl.when(jnp.logical_not(comes))
            def _():
                recv_ref[slot] = jnp.zeros(recv_ref.shape[1:], recv_ref.dtype)

    loads[0].wait()
    loads[1].wait()
    starts = []
    for _, _, _, (kind, row) in plan:
        starts.append(adj_ref[row, 1] if kind == "adj" else border_ref[0, row])
    for part, (load, whole) in enumerate(((loads[2], k_ref), (loads[3], v_ref))):
        load.wait()
        for slot in range(len(plan)):
            for head in range(heads):
                send_ref[slot, part, head] = whole[
                    starts[slot], :, head * HD : (head + 1) * HD
                ]

    arrivals = sum(1 if comes is None else comes.astype(jnp.int32) for _, _, comes, _ in plan)
    pl.semaphore_wait(barrier, arrivals)

    def transfer(slot, part, group):
        at = (slot, part, pl.ds(group * GROUP, GROUP))
        return pltpu.make_async_remote_copy(
            src_ref=send_ref.at[at],
            dst_ref=recv_ref.at[at],
            send_sem=send_sem.at[slot, part, group],
            recv_sem=recv_sem.at[slot, part, group],
            device_id=plan[slot][0],
            device_id_type=MESH,
        )

    for part in range(2):
        for group in range(groups):
            for slot, (_, sends, _, _) in enumerate(plan):
                @when(sends)
                def _():
                    transfer(slot, part, group).start()

    loads[4].wait()
    own = []
    for head in range(heads):
        columns = slice(head * HD, (head + 1) * HD)
        scores = weigh(q_ref[:, columns], k_ref[:, :, columns].reshape(rows, HD))
        most = jnp.max(scores, axis=1, keepdims=True)
        weights = jnp.exp2(scores - most)
        total = jnp.sum(weights, axis=1, keepdims=True)
        acc_ref[head] = jnp.dot(
            weights.astype(jnp.bfloat16), v_ref[:, :, columns].reshape(rows, HD), preferred_element_type=jnp.float32
        )
        own.append((most, total))

    for group in range(groups):
        for slot, (_, _, comes, _) in enumerate(plan):
            @when(comes)
            def _():
                transfer(slot, 0, group).wait_recv()
        for head in range(group * GROUP, (group + 1) * GROUP):
            columns = slice(head * HD, (head + 1) * HD)
            pieces = [own[head]]
            for slot, (_, _, comes, _) in enumerate(plan):
                scores = weigh(q_ref[:, columns], recv_ref[slot, 0, head])
                if comes is not None:
                    scores = scores + jnp.where(comes, 0.0, masked_score).astype(jnp.float32)
                most = jnp.max(scores, axis=1, keepdims=True)
                weights = jnp.exp2(scores - most)
                total = jnp.sum(weights, axis=1, keepdims=True)
                weights_ref[head, slot] = weights.astype(jnp.bfloat16)
                pieces.append((most, total))
            largest = functools.reduce(jnp.maximum, [most for most, _ in pieces])
            factors = [jnp.exp2(most - largest) for most, _ in pieces]
            denominator = sum(factor * total for factor, (_, total) in zip(factors, pieces))
            acc_ref[head] = acc_ref[head] * (factors[0] / denominator)
            for slot in range(len(plan)):
                gain_ref[head, slot] = jnp.broadcast_to(
                    factors[slot + 1] / denominator, (rows, HD)
                )

    for group in range(groups):
        for slot, (_, _, comes, _) in enumerate(plan):
            @when(comes)
            def _():
                transfer(slot, 1, group).wait_recv()
        for head in range(group * GROUP, (group + 1) * GROUP):
            result = acc_ref[head]
            for slot in range(len(plan)):
                result = result + gain_ref[head, slot] * jnp.dot(
                    weights_ref[head, slot], recv_ref[slot, 1, head], preferred_element_type=jnp.float32
                )
            out_ref[:, head * HD : (head + 1) * HD] = result.astype(out_ref.dtype)

    for part in range(2):
        for group in range(groups):
            for slot, (_, sends, _, _) in enumerate(plan):
                @when(sends)
                def _():
                    transfer(slot, part, group).wait_send()


def per_device(queries, keys, values, adj_mask, border_blocks):
    rows, width = queries.shape[2:]
    heads = width // HD
    slab_count, band_count = lax.axis_size("tm"), lax.axis_size("band")
    sources = (2 if slab_count > 1 else 0) + min(band_count - 1, 2)
    assert rows == 2 * BLK and adj_mask.shape[3] == 2 and border_blocks.shape[3] == 1
    block_sems = pltpu.SemaphoreType.DMA((sources, 2, heads // GROUP))
    attended = pl.pallas_call(
        functools.partial(kernel, slab_count, band_count),
        out_shape=pltpu.VMEM((rows, width), jnp.bfloat16),
        in_specs=[pl.BlockSpec(memory_space=pl.ANY)] * 5,
        out_specs=pl.BlockSpec(memory_space=pltpu.VMEM),
        scratch_shapes=[
            pltpu.VMEM((rows, width), jnp.bfloat16),
            pltpu.VMEM((rows // BLK, BLK, width), jnp.bfloat16),
            pltpu.VMEM((rows // BLK, BLK, width), jnp.bfloat16),
            pltpu.SMEM(adj_mask.shape[2:], jnp.int32),
            pltpu.SMEM(border_blocks.shape[:1:-1], jnp.int32),
            pltpu.VMEM((sources, 2, heads, BLK, HD), jnp.bfloat16),
            pltpu.VMEM((sources, 2, heads, BLK, HD), jnp.bfloat16),
            pltpu.VMEM((heads, rows, HD), jnp.float32),
            pltpu.VMEM((heads, sources, rows, BLK), jnp.bfloat16),
            pltpu.VMEM((heads, sources, rows, HD), jnp.float32),
            pltpu.SemaphoreType.DMA((5,)),
            block_sems,
            block_sems,
        ],
        compiler_params=pltpu.CompilerParams(collective_id=0, has_side_effects=True),
        name="radial_attention",
    )(
        queries[0, 0],
        keys.reshape(rows // BLK, BLK, width),
        values.reshape(rows // BLK, BLK, width),
        adj_mask[0, 0], border_blocks[0, 0].T,
    )
    return attended[None, None]


def solution(mesh):
    placed = (
        P(("clip", "tm"), "band", None, "head"),
        P(("clip", "tm"), "band", None, "head"),
        P(("clip", "tm"), "band", None, "head"),
        P(("clip", "tm"), "band", None, None),
        P(("clip", "tm"), "band", None, None),
    )
    return jax.shard_map(
        per_device,
        mesh=mesh,
        in_specs=placed,
        out_specs=P(("clip", "tm"), "band", None, "head"),
        check_vma=False,
    )
```

```python
import functools
import math

import jax
import jax.numpy as jnp
from jax import lax
from jax.experimental import pallas as pl
from jax.experimental.pallas import tpu as pltpu
from jax.sharding import PartitionSpec as P

BLK = 128
HD = 128

masked_score = -1e30
SCALE2 = math.log2(math.e) / math.sqrt(HD)
MESH = pl.DeviceIdType.MESH


def routes(slab_count, band_count):
    slab, band = lax.axis_index("tm"), lax.axis_index("band")
    found = []
    if slab_count > 1:
        found.append(({"tm": slab + 1}, slab < slab_count - 1, None, slab > 0, ("adj", 0)))
        found.append(({"tm": slab - 1}, None, slab > 0, slab < slab_count - 1, ("adj", 1)))
    if band_count == 2:
        found.append(({"band": 1 - band}, band == 0, band == 1, None, ("border", 1 - band)))
    elif band_count > 2:
        found.append(({"band": band + 1}, band < band_count - 1, None, band > 0, ("border", 1)))
        found.append(({"band": band - 1}, None, band > 0, band < band_count - 1, ("border", 0)))
    return found


def when(condition):
    return (lambda body: body()) if condition is None else pl.when(condition)


def chunks_of(heads):
    half = heads // 2
    return (
        [(0, half), (half, heads - half)],
        [(0, half), (half, heads - half - 1), (heads - 1, 1)],
    )


def weigh(query, key):
    scores = lax.dot_general(
        query, key, (((1,), (1,)), ((), ())), preferred_element_type=jnp.float32
    )
    return scores * SCALE2


def kernel(
    slab_count, band_count, q_hbm, k_hbm, v_hbm, adj_hbm, border_hbm, out_ref,
    q_ref, k_ref, v_ref, adj_ref, border_ref, send_ref, recv_ref, acc_ref, weights_ref,
    gain_ref, load_sem, here_sem, send_sem, recv_sem,
):
    plan = routes(slab_count, band_count)
    rows, width = q_ref.shape
    heads = width // HD

    neighbours = []
    for axis, count in (("tm", slab_count), ("band", band_count)):
        if count > 1:
            index = lax.axis_index(axis)
            neighbours.append((axis, index, index > 0, index < count - 1))

    barrier = pltpu.get_barrier_semaphore()
    for axis, index, _, has_upper in neighbours:
        @pl.when(has_upper)
        def _():
            pl.semaphore_signal(barrier, inc=1, device_id={axis: index + 1}, device_id_type=MESH)

    picks = []
    for number, (source, target) in enumerate(((adj_hbm, adj_ref), (border_hbm, border_ref))):
        picks.append(pltpu.make_async_copy(source, target, load_sem.at[number]))
    for pick in picks:
        pick.start()
    loads = [
        pltpu.make_async_copy(source, target, load_sem.at[2 + number])
        for number, (source, target) in enumerate(((k_hbm, k_ref), (v_hbm, v_ref), (q_hbm, q_ref)))
    ]
    loads[0].start()

    chunks = chunks_of(heads)

    def transfer(slot, part, group):
        at = (slot, part, pl.ds(*chunks[part][group]))
        return pltpu.make_async_remote_copy(
            src_ref=send_ref.at[at],
            dst_ref=recv_ref.at[at],
            send_sem=send_sem.at[slot, part, group],
            recv_sem=recv_sem.at[slot, part, group],
            device_id=plan[slot][0],
            device_id_type=MESH,
        )

    def send(part, downward):
        for group in range(len(chunks[part])):
            for slot, (_, up, down, _, _) in enumerate(plan):
                sends = down if downward else up
                if sends is not None:
                    @pl.when(sends)
                    def _():
                        transfer(slot, part, group).start()

    arrivals = sum(lower.astype(jnp.int32) for _, _, lower, _ in neighbours)

    @pl.when(arrivals > 0)
    def _():
        pl.semaphore_wait(barrier, arrivals)

    for number, (axis, index, has_lower, _) in enumerate(neighbours):
        @pl.when(has_lower)
        def _():
            pl.semaphore_signal(
                here_sem.at[number], inc=1, device_id={axis: index - 1}, device_id_type=MESH
            )

    for pick in picks:
        pick.wait()
    blocks = [
        adj_ref[row, 1] if kind == "adj" else border_ref[0, row] for _, _, _, _, (kind, row) in plan
    ]
    for part, whole in enumerate((k_ref, v_ref)):
        loads[part].wait()
        if part == 0:
            loads[1].start()
            loads[2].start()
        for slot in range(len(plan)):
            for head in range(heads):
                send_ref[slot, part, head] = whole[blocks[slot], :, head * HD : (head + 1) * HD]
        send(part, True)
    for number, (_, _, _, has_upper) in enumerate(neighbours):
        @pl.when(has_upper)
        def _():
            pl.semaphore_wait(here_sem.at[number], 1)
    for part in range(2):
        send(part, False)

    for slot, (_, _, _, comes, _) in enumerate(plan):
        if comes is not None:
            @pl.when(jnp.logical_not(comes))
            def _():
                recv_ref[slot] = jnp.zeros(recv_ref.shape[1:], recv_ref.dtype)

    loads[2].wait()
    own = []
    for head in range(heads):
        columns = slice(head * HD, (head + 1) * HD)
        scores = weigh(q_ref[:, columns], k_ref[:, :, columns].reshape(rows, HD))
        most = jnp.max(scores, axis=1, keepdims=True)
        weights = jnp.exp2(scores - most)
        total = jnp.sum(weights, axis=1, keepdims=True)
        acc_ref[head] = jnp.dot(
            weights.astype(jnp.bfloat16), v_ref[:, :, columns].reshape(rows, HD), preferred_element_type=jnp.float32
        )
        own.append((most, total))

    for group, (start, size) in enumerate(chunks[0]):
        for slot, (_, _, _, comes, _) in enumerate(plan):
            @when(comes)
            def _():
                transfer(slot, 0, group).wait_recv()
        for head in range(start, start + size):
            columns = slice(head * HD, (head + 1) * HD)
            pieces = [own[head]]
            for slot, (_, _, _, comes, _) in enumerate(plan):
                scores = weigh(q_ref[:, columns], recv_ref[slot, 0, head])
                if comes is not None:
                    scores = scores + jnp.where(comes, 0.0, masked_score).astype(jnp.float32)
                most = jnp.max(scores, axis=1, keepdims=True)
                weights = jnp.exp2(scores - most)
                total = jnp.sum(weights, axis=1, keepdims=True)
                weights_ref[head, slot] = weights.astype(jnp.bfloat16)
                pieces.append((most, total))
            largest = functools.reduce(jnp.maximum, [most for most, _ in pieces])
            factors = [jnp.exp2(most - largest) for most, _ in pieces]
            denominator = sum(factor * total for factor, (_, total) in zip(factors, pieces))
            acc_ref[head] = acc_ref[head] * (factors[0] / denominator)
            for slot in range(len(plan)):
                gain_ref[head, slot] = jnp.broadcast_to(
                    factors[slot + 1] / denominator, (rows, HD)
                )

    for group, (start, size) in enumerate(chunks[1]):
        for slot, (_, _, _, comes, _) in enumerate(plan):
            @when(comes)
            def _():
                transfer(slot, 1, group).wait_recv()
        for head in range(start, start + size):
            result = acc_ref[head]
            for slot in range(len(plan)):
                result = result + gain_ref[head, slot] * jnp.dot(
                    weights_ref[head, slot], recv_ref[slot, 1, head], preferred_element_type=jnp.float32
                )
            out_ref[:, head * HD : (head + 1) * HD] = result.astype(out_ref.dtype)

    for part in range(2):
        for group in range(len(chunks[part])):
            for slot, (_, up, down, _, _) in enumerate(plan):
                sends = down if up is None else up if down is None else None

                @when(sends)
                def _():
                    transfer(slot, part, group).wait_send()


def per_device(queries, keys, values, adj_mask, border_blocks):
    rows, width = queries.shape[2:]
    heads = width // HD
    slab_count, band_count = lax.axis_size("tm"), lax.axis_size("band")
    sources = (2 if slab_count > 1 else 0) + min(band_count - 1, 2)
    assert rows == 2 * BLK and adj_mask.shape[3] == 2 and border_blocks.shape[3] == 1
    block_sems = pltpu.SemaphoreType.DMA((sources, 2, max(map(len, chunks_of(heads)))))
    attended = pl.pallas_call(
        functools.partial(kernel, slab_count, band_count),
        out_shape=pltpu.VMEM((rows, width), jnp.bfloat16),
        in_specs=[pl.BlockSpec(memory_space=pl.ANY)] * 5,
        out_specs=pl.BlockSpec(memory_space=pltpu.VMEM),
        scratch_shapes=[
            pltpu.VMEM((rows, width), jnp.bfloat16),
            pltpu.VMEM((rows // BLK, BLK, width), jnp.bfloat16),
            pltpu.VMEM((rows // BLK, BLK, width), jnp.bfloat16),
            pltpu.SMEM(adj_mask.shape[2:], jnp.int32),
            pltpu.SMEM(border_blocks.shape[:1:-1], jnp.int32),
            pltpu.VMEM((sources, 2, heads, BLK, HD), jnp.bfloat16),
            pltpu.VMEM((sources, 2, heads, BLK, HD), jnp.bfloat16),
            pltpu.VMEM((heads, rows, HD), jnp.float32),
            pltpu.VMEM((heads, sources, rows, BLK), jnp.bfloat16),
            pltpu.VMEM((heads, sources, rows, HD), jnp.float32),
            pltpu.SemaphoreType.DMA((5,)),
            pltpu.SemaphoreType.REGULAR((max(1, (slab_count > 1) + (band_count > 1)),)),
            block_sems,
            block_sems,
        ],
        compiler_params=pltpu.CompilerParams(collective_id=0, has_side_effects=True),
        name="radial_attention",
    )(
        queries[0, 0],
        keys.reshape(rows // BLK, BLK, width),
        values.reshape(rows // BLK, BLK, width),
        adj_mask[0, 0], border_blocks[0, 0].T,
    )
    return attended[None, None]


def solution(mesh):
    placed = (
        P(("clip", "tm"), "band", None, "head"),
        P(("clip", "tm"), "band", None, "head"),
        P(("clip", "tm"), "band", None, "head"),
        P(("clip", "tm"), "band", None, None),
        P(("clip", "tm"), "band", None, None),
    )
    return jax.shard_map(
        per_device,
        mesh=mesh,
        in_specs=placed,
        out_specs=P(("clip", "tm"), "band", None, "head"),
        check_vma=False,
    )
```

```python
import functools
import math

import jax
import jax.numpy as jnp
from jax import lax
from jax.experimental import pallas as pl
from jax.experimental.pallas import tpu as pltpu
from jax.sharding import PartitionSpec as P

BLK = 128
HD = 128

masked_score = -1e30
SCALE2 = math.log2(math.e) / math.sqrt(HD)
MESH = pl.DeviceIdType.MESH


def routes(slab_count, band_count):
    slab, band = lax.axis_index("tm"), lax.axis_index("band")
    found = []
    if slab_count > 1:
        found.append(({"tm": slab + 1}, slab < slab_count - 1, None, slab > 0, ("adj", 0)))
        found.append(({"tm": slab - 1}, None, slab > 0, slab < slab_count - 1, ("adj", 1)))
    if band_count == 2:
        found.append(({"band": 1 - band}, band == 0, band == 1, None, ("border", 1 - band)))
    elif band_count > 2:
        found.append(({"band": band + 1}, band < band_count - 1, None, band > 0, ("border", 1)))
        found.append(({"band": band - 1}, None, band > 0, band < band_count - 1, ("border", 0)))
    return found


def when(condition):
    return (lambda body: body()) if condition is None else pl.when(condition)


def chunks_of(heads):
    return (
        [(0, heads)],
        [(0, heads - 1), (heads - 1, 1)],
    )


def weigh(query, key):
    scores = lax.dot_general(
        query, key, (((1,), (1,)), ((), ())), preferred_element_type=jnp.float32
    )
    return scores * SCALE2


def kernel(
    slab_count, band_count, q_hbm, k_hbm, v_hbm, adj_hbm, border_hbm, out_ref,
    q_ref, k_ref, v_ref, adj_ref, border_ref, send_ref, recv_ref, acc_ref, weights_ref,
    gain_ref, load_sem, here_sem, send_sem, recv_sem,
):
    plan = routes(slab_count, band_count)
    rows, width = q_ref.shape
    heads = width // HD

    neighbours = []
    for axis, count in (("tm", slab_count), ("band", band_count)):
        if count > 1:
            index = lax.axis_index(axis)
            neighbours.append((axis, index, index > 0, index < count - 1))

    barrier = pltpu.get_barrier_semaphore()
    for axis, index, _, has_upper in neighbours:
        @pl.when(has_upper)
        def _():
            pl.semaphore_signal(barrier, inc=1, device_id={axis: index + 1}, device_id_type=MESH)

    picks = []
    for number, (source, target) in enumerate(((adj_hbm, adj_ref), (border_hbm, border_ref))):
        picks.append(pltpu.make_async_copy(source, target, load_sem.at[number]))
    for pick in picks:
        pick.start()
    loads = [
        pltpu.make_async_copy(source, target, load_sem.at[2 + number])
        for number, (source, target) in enumerate(((k_hbm, k_ref), (v_hbm, v_ref), (q_hbm, q_ref)))
    ]
    loads[0].start()

    chunks = chunks_of(heads)

    def transfer(slot, part, group):
        at = (slot, part, pl.ds(*chunks[part][group]))
        return pltpu.make_async_remote_copy(
            src_ref=send_ref.at[at],
            dst_ref=recv_ref.at[at],
            send_sem=send_sem.at[slot, part, group],
            recv_sem=recv_sem.at[slot, part, group],
            device_id=plan[slot][0],
            device_id_type=MESH,
        )

    def send(part, downward):
        for group in range(len(chunks[part])):
            for slot, (_, up, down, _, _) in enumerate(plan):
                sends = down if downward else up
                if sends is not None:
                    @pl.when(sends)
                    def _():
                        transfer(slot, part, group).start()

    arrivals = sum(lower.astype(jnp.int32) for _, _, lower, _ in neighbours)

    @pl.when(arrivals > 0)
    def _():
        pl.semaphore_wait(barrier, arrivals)

    for number, (axis, index, has_lower, _) in enumerate(neighbours):
        @pl.when(has_lower)
        def _():
            pl.semaphore_signal(
                here_sem.at[number], inc=1, device_id={axis: index - 1}, device_id_type=MESH
            )

    for pick in picks:
        pick.wait()
    blocks = [
        adj_ref[row, 1] if kind == "adj" else border_ref[0, row] for _, _, _, _, (kind, row) in plan
    ]
    for part, whole in enumerate((k_ref, v_ref)):
        loads[part].wait()
        if part == 0:
            loads[1].start()
            loads[2].start()
        for slot in range(len(plan)):
            for head in range(heads):
                send_ref[slot, part, head] = whole[blocks[slot], :, head * HD : (head + 1) * HD]
        send(part, True)
    for number, (_, _, _, has_upper) in enumerate(neighbours):
        @pl.when(has_upper)
        def _():
            pl.semaphore_wait(here_sem.at[number], 1)
    for part in range(2):
        send(part, False)

    for slot, (_, _, _, comes, _) in enumerate(plan):
        if comes is not None:
            @pl.when(jnp.logical_not(comes))
            def _():
                recv_ref[slot] = jnp.zeros(recv_ref.shape[1:], recv_ref.dtype)

    loads[2].wait()
    own = []
    for head in range(heads):
        columns = slice(head * HD, (head + 1) * HD)
        scores = weigh(q_ref[:, columns], k_ref[:, :, columns].reshape(rows, HD))
        most = jnp.max(scores, axis=1, keepdims=True)
        weights = jnp.exp2(scores - most)
        total = jnp.sum(weights, axis=1, keepdims=True)
        acc_ref[head] = jnp.dot(
            weights.astype(jnp.bfloat16), v_ref[:, :, columns].reshape(rows, HD), preferred_element_type=jnp.float32
        )
        own.append((most, total))

    for group, (start, size) in enumerate(chunks[0]):
        for slot, (_, _, _, comes, _) in enumerate(plan):
            @when(comes)
            def _():
                transfer(slot, 0, group).wait_recv()
        for head in range(start, start + size):
            columns = slice(head * HD, (head + 1) * HD)
            pieces = [own[head]]
            for slot, (_, _, _, comes, _) in enumerate(plan):
                scores = weigh(q_ref[:, columns], recv_ref[slot, 0, head])
                if comes is not None:
                    scores = scores + jnp.where(comes, 0.0, masked_score).astype(jnp.float32)
                most = jnp.max(scores, axis=1, keepdims=True)
                weights = jnp.exp2(scores - most)
                total = jnp.sum(weights, axis=1, keepdims=True)
                weights_ref[head, slot] = weights.astype(jnp.bfloat16)
                pieces.append((most, total))
            largest = functools.reduce(jnp.maximum, [most for most, _ in pieces])
            factors = [jnp.exp2(most - largest) for most, _ in pieces]
            denominator = sum(factor * total for factor, (_, total) in zip(factors, pieces))
            acc_ref[head] = acc_ref[head] * (factors[0] / denominator)
            for slot in range(len(plan)):
                gain_ref[head, slot] = jnp.broadcast_to(
                    factors[slot + 1] / denominator, (rows, HD)
                )

    for group, (start, size) in enumerate(chunks[1]):
        for slot, (_, _, _, comes, _) in enumerate(plan):
            @when(comes)
            def _():
                transfer(slot, 1, group).wait_recv()
        for head in range(start, start + size):
            result = acc_ref[head]
            for slot in range(len(plan)):
                result = result + gain_ref[head, slot] * jnp.dot(
                    weights_ref[head, slot], recv_ref[slot, 1, head], preferred_element_type=jnp.float32
                )
            out_ref[:, head * HD : (head + 1) * HD] = result.astype(out_ref.dtype)

    for part in range(2):
        for group in range(len(chunks[part])):
            for slot, (_, up, down, _, _) in enumerate(plan):
                sends = down if up is None else up if down is None else None

                @when(sends)
                def _():
                    transfer(slot, part, group).wait_send()


def per_device(queries, keys, values, adj_mask, border_blocks):
    rows, width = queries.shape[2:]
    heads = width // HD
    slab_count, band_count = lax.axis_size("tm"), lax.axis_size("band")
    sources = (2 if slab_count > 1 else 0) + min(band_count - 1, 2)
    assert rows == 2 * BLK and adj_mask.shape[3] == 2 and border_blocks.shape[3] == 1
    block_sems = pltpu.SemaphoreType.DMA((sources, 2, max(map(len, chunks_of(heads)))))
    attended = pl.pallas_call(
        functools.partial(kernel, slab_count, band_count),
        out_shape=pltpu.VMEM((rows, width), jnp.bfloat16),
        in_specs=[pl.BlockSpec(memory_space=pl.ANY)] * 5,
        out_specs=pl.BlockSpec(memory_space=pltpu.VMEM),
        scratch_shapes=[
            pltpu.VMEM((rows, width), jnp.bfloat16),
            pltpu.VMEM((rows // BLK, BLK, width), jnp.bfloat16),
            pltpu.VMEM((rows // BLK, BLK, width), jnp.bfloat16),
            pltpu.SMEM(adj_mask.shape[2:], jnp.int32),
            pltpu.SMEM(border_blocks.shape[:1:-1], jnp.int32),
            pltpu.VMEM((sources, 2, heads, BLK, HD), jnp.bfloat16),
            pltpu.VMEM((sources, 2, heads, BLK, HD), jnp.bfloat16),
            pltpu.VMEM((heads, rows, HD), jnp.float32),
            pltpu.VMEM((heads, sources, rows, BLK), jnp.bfloat16),
            pltpu.VMEM((heads, sources, rows, HD), jnp.float32),
            pltpu.SemaphoreType.DMA((5,)),
            pltpu.SemaphoreType.REGULAR((max(1, (slab_count > 1) + (band_count > 1)),)),
            block_sems,
            block_sems,
        ],
        compiler_params=pltpu.CompilerParams(collective_id=0, has_side_effects=True),
        name="radial_attention",
    )(
        queries[0, 0],
        keys.reshape(rows // BLK, BLK, width),
        values.reshape(rows // BLK, BLK, width),
        adj_mask[0, 0], border_blocks[0, 0].T,
    )
    return attended[None, None]


def solution(mesh):
    placed = (
        P(("clip", "tm"), "band", None, "head"),
        P(("clip", "tm"), "band", None, "head"),
        P(("clip", "tm"), "band", None, "head"),
        P(("clip", "tm"), "band", None, None),
        P(("clip", "tm"), "band", None, None),
    )
    return jax.shard_map(
        per_device,
        mesh=mesh,
        in_specs=placed,
        out_specs=P(("clip", "tm"), "band", None, "head"),
        check_vma=False,
    )
```
